32 devices in a mesh: groups: 2 (over x), blk: 16 (over z, y, core).
Axes of the slice: x: 2, y: 2, z: 4, core: 2. Of those that a mesh axis runs over, the one named last changes fastest.
Arguments:
- tokens: bfloat16 [2048, 4096], P(('groups', 'blk')), parts along dimension 0, may hold values from -9 to 9, as said below
- blocks: bfloat16 [16, 7, 128, 128], P('blk'), may hold values from -0.5 to 0.5
- counts: int32 [2, 8], replicated, may hold values from 1 to 7, 48 in all within a row
- block_rows: int32 [16, 7], replicated, may hold values from 0 to 31
- block_cols: int32 [16, 7], replicated, may hold values from 0 to 111
Outputs:
- up: bfloat16 [2048, 14336], P(('groups', 'blk')), parts along dimension 0
- col_rms: float32 [28672], P('groups'), parts along dimension 0
The draws below stay inside these ranges and needn't reach their ends.
There are 2 independent parts, one for each index of `groups`. The reference program is written for one: setup_inputs(seed, part) draws one part's arguments, and reference() takes and returns one part's arrays. A program takes and returns all parts, laid end to end along the dimension named above; an argument that names none is the same for every part. Nothing has to cross between parts.
Inputs may be any that keep to these rules, and one draw needn't show every extreme that they name: `tokens`: scale of a token's entries grows with its position in the sequence. `counts`: each row sums to 48, and each row has an entry equal to 7. `block_rows`: slots at or past an owner's count carry no block and are ignored, whatever they hold. `block_cols`: slots at or past an owner's count are ignored.
All inputs are finite; a program needn't handle non-finite values.
Results may differ from the reference program's by a relative error of at most 0.001.
Values may be sent and summed in bfloat16 or wider, within the bound.
No kernel may reach another device: no remote copies, remote signals or barrier semaphores. Data moves between devices by JAX's collectives and lax.ppermute only.
A program may use at most 192 MiB of HBM per device.

```python
import math
import jax
import jax.numpy as jnp
import numpy as np
from jax import lax

D = 4096
FFW = 14336
BS = 128
MAXB = 7
AVG = 6
BAL = 8
OWNERS = 16
TOKENS = 1024
ROWB = 32
COLB = 112


def draw_tokens(key, part):
    position = jnp.arange(TOKENS, dtype=jnp.float32)[:, None] / TOKENS
    values = jnp.clip(jax.random.normal(key, (TOKENS, D), jnp.float32), -5.0, 5.0)
    scale = jnp.sqrt(1.0 + 2.0 * position)
    return (values * scale).astype(jnp.bfloat16)


def place_ends(array, stream_key, smallest, largest):
    longest = array.shape.index(max(array.shape))
    spots = []
    for shift in (0, 1):
        where = [jax.random.randint(jax.random.fold_in(stream_key, axis), (), 0, length) for axis, length in enumerate(array.shape)]
        where[longest] = (where[longest] + shift) % array.shape[longest]
        spots.append(tuple(where))
    return array.at[spots[0]].set(smallest).at[spots[1]].set(largest)


def steps_of(rng, dims, cuts, low, top_value):
    def one(axis_at, blocks):
        heights = jax.random.uniform(jax.random.fold_in(jax.random.fold_in(rng, 6), axis_at), (blocks,), jnp.float32, low / len(cuts), top_value / len(cuts))
        return jnp.repeat(jnp.exp(heights), dims[axis_at] // blocks).reshape((-1,) + (1,) * (len(dims) - axis_at - 1))

    loudness = one(*cuts[0])
    for cut in cuts[1:]:
        loudness = loudness * one(*cut)
    return loudness


def profile(count, total, limit, slope):
    portions = [(1 << 20) // math.isqrt(rank ** slope) + 1 for rank in range(2, count + 1)]
    rest, given = total - limit - (count - 1), [1] * (count - 1)
    while rest > 0:
        candidates = [i for i in range(count - 1) if given[i] < limit]
        mass, budget = sum([portions[i] for i in candidates]), rest
        for i in candidates:
            addition = min(limit - given[i], max(1, budget * portions[i] // mass), rest)
            given[i] = given[i] + addition
            rest = rest - addition
    return np.array([limit] + given)


def uneven(rng, number_of, total, most, skew):
    if number_of == 2:
        one = jax.random.randint(rng, (), max(1, total - most), min(most, total - 1) + 1)
        return jnp.stack([one, total - one])
    lengths = jnp.asarray(profile(number_of, total, most, skew), jnp.int32)
    pairs = (number_of - 1) // 2
    source_of, receiver = lengths[1:1 + 2 * pairs:2], lengths[2:2 + 2 * pairs:2]
    room = jnp.minimum(source_of - 1, most - receiver)
    shifted = jax.random.randint(jax.random.fold_in(rng, 1), (pairs,), 0, 1 << 20) % (room + 1)
    lengths = lengths.at[1:1 + 2 * pairs:2].set(source_of - shifted).at[2:2 + 2 * pairs:2].set(receiver + shifted)
    return lengths[jax.random.permutation(jax.random.fold_in(rng, 2), number_of)]


def noise(own_key, dims, spread, limit, shards=(), kind=jnp.bfloat16):
    entries = jax.random.normal(own_key, dims, jnp.float32) * spread
    if len(shards) > 0:
        entries = steps_of(own_key, dims, shards, -0.22, 0.18) * entries
    return jnp.clip(entries, min=-limit, max=limit).astype(kind)


def setup_inputs(seed: int = 0, part: int = 0) -> dict:
    splits = jax.random.split(jax.random.key(seed), 6)
    own_keys = jax.random.split(jax.random.fold_in(splits[5], part), 6)
    tokens = draw_tokens(jax.random.fold_in(jax.random.fold_in(splits[5], part), 71), part)
    blocks = noise(splits[1], (OWNERS, MAXB, BS, BS), (OWNERS * AVG * BS * BS // FFW) ** -0.5, 0.5, ((0, 16),))
    counts = jax.vmap(lambda own: uneven(own, BAL, BAL * AVG, MAXB, 2))(jax.random.split(splits[2], (OWNERS // BAL))).reshape((OWNERS // BAL, BAL)).astype(jnp.int32)
    block_rows = place_ends(jax.random.randint(splits[3], (OWNERS, MAXB), 0, ROWB), jax.random.fold_in(splits[3], 1), 0, ROWB - 1).astype(jnp.int32)
    block_cols = place_ends(jax.random.randint(splits[4], (OWNERS, MAXB), 0, COLB), jax.random.fold_in(splits[4], 1), 0, COLB - 1).astype(jnp.int32)
    return dict(tokens=tokens, blocks=blocks, counts=counts, block_rows=block_rows, block_cols=block_cols)


def reference(tokens, blocks, counts, block_rows, block_cols):
    flat = counts.reshape(-1)

    def owner_step(owner, acc):

        def slot_step(slot, inner):
            row = (block_rows[owner, slot] * BS).astype(jnp.int32)
            col = (block_cols[owner, slot] * BS).astype(jnp.int32)
            chosen = lax.dynamic_slice_in_dim(tokens, row, BS, 1)
            term = jnp.dot(chosen, blocks[owner, slot], preferred_element_type=jnp.float32)
            current = lax.dynamic_slice_in_dim(inner, col, BS, 1)
            return lax.dynamic_update_slice_in_dim(inner, current + term, col, 1)
        return lax.fori_loop(0, flat[owner], slot_step, acc)
    product = lax.fori_loop(0, OWNERS, owner_step, jnp.zeros((TOKENS, FFW), jnp.float32))
    up = product.astype(jnp.bfloat16)
    col_rms = jnp.sqrt(lax.optimization_barrier(jnp.sum(product * product, axis=0)) / TOKENS + 1e-06)
    return (up, col_rms)
```

```python
import functools

import jax
import jax.numpy as jnp
from jax import lax
from jax.experimental import pallas as pl
from jax.experimental.pallas import tpu as pltpu
from jax.sharding import PartitionSpec as P


def flip(value, bit, size):
    return lax.ppermute(value, "blk", [(i, i ^ bit) for i in range(size)])


def bits_of(size):
    bits = []
    bit = 1
    while bit < size:
        bits.append(bit)
        bit *= 2
    return bits


def gather_lists(blocks, size):
    held = {0: blocks}
    for bit in reversed(bits_of(size)):
        for key in list(held):
            held[key ^ bit] = flip(held[key], bit, size)
    return held


def kernel(keys, me_ref, counts_ref, rows_ref, cols_ref, tokens_ref, *rest):
    lists = rest[: len(keys)]
    up_ref, squares_ref, weights, acc, sems = rest[len(keys) :]
    slots, edge = weights.shape[1], weights.shape[2]
    col_blocks = squares_ref.shape[0]
    me = me_ref[0]
    per_row = counts_ref.shape[1]

    def copy(at):
        return pltpu.make_async_copy(lists[at], weights.at[at], sems.at[at])

    for at in range(len(keys)):
        copy(at).start()
    zero = jnp.zeros(acc.shape[1:], jnp.float32)

    @pl.loop(0, col_blocks)
    def _(c):
        acc[c] = zero

    for at, key in enumerate(keys):
        copy(at).wait()
        owner = me ^ key
        count = counts_ref[owner // per_row, owner % per_row]
        for slot in range(slots):
            live = slot < count
            row = jnp.where(live, rows_ref[owner, slot], 0)
            col = jnp.where(live, cols_ref[owner, slot], col_blocks)
            picked = tokens_ref[:, pl.ds(pl.multiple_of(row * edge, edge), edge)]
            term = jnp.dot(picked, weights[at, slot], preferred_element_type=jnp.float32)
            acc[col] += term

    for c in range(col_blocks):
        value = acc[c]
        up_ref[:, c * edge : (c + 1) * edge] = value.astype(up_ref.dtype)
        squares_ref[c] = jnp.sum(value * value, axis=0)


def per_device(width, size, tokens, blocks, counts, block_rows, block_cols):
    tok_count = tokens.shape[0]
    slots, edge = blocks.shape[1], blocks.shape[2]
    col_blocks = width // edge
    owned = blocks.reshape(slots, edge, edge)
    held = gather_lists(owned, size)
    keys = tuple(held)
    me = lax.axis_index("blk").astype(jnp.int32).reshape(1)
    smem = pl.BlockSpec(memory_space=pltpu.SMEM)
    vmem = pl.BlockSpec(memory_space=pltpu.VMEM)
    up, squares = pl.pallas_call(
        functools.partial(kernel, keys),
        out_shape=(
            jax.ShapeDtypeStruct((tok_count, width), jnp.bfloat16),
            jax.ShapeDtypeStruct((col_blocks, edge), jnp.float32),
        ),
        in_specs=[smem] * 4 + [vmem] + [pl.BlockSpec(memory_space=pl.ANY)] * len(keys),
        out_specs=(vmem, vmem),
        scratch_shapes=[
            pltpu.VMEM((len(keys), slots, edge, edge), jnp.bfloat16),
            pltpu.VMEM((col_blocks + 1, tok_count, edge), jnp.float32),
            pltpu.SemaphoreType.DMA((len(keys),)),
        ],
        compiler_params=pltpu.CompilerParams(vmem_limit_bytes=56 << 20),
    )(me, counts, block_rows, block_cols, tokens, *[held[k] for k in keys])
    for bit in bits_of(size):
        squares = squares + flip(squares, bit, size)
    squares = squares.reshape(-1)
    col_rms = jnp.sqrt(squares / (tok_count * size) + 1e-06)
    return (up, col_rms)


FFW = 14336


def solution(mesh):
    placed = (P(("groups", "blk"), None), P("blk", None, None, None), P(), P(), P())
    return jax.shard_map(
        functools.partial(per_device, FFW, mesh.shape["blk"]),
        mesh=mesh,
        in_specs=placed,
        out_specs=(P(("groups", "blk"), None), P("groups")),
        check_vma=False,
    )
```
